256 devices in a mesh: row: 16 (over z_lo, y, core), col: 16 (over x, z_hi).
Axes of the slice: x: 4, y: 4, z: 8 (z_hi: 4, z_lo: 2; z = z_hi * 2 + z_lo), core: 2. Of those that a mesh axis runs over, the one named last changes fastest.
Arguments:
- density: float32 [16, 16, 7, 2, 128, 128], P('row', 'col'), may hold values from -1 to 2, as said below
- hamiltonian: float32 [16, 16, 7, 2, 128, 128], P('row', 'col'), may hold values from -2 to 4, as said below
- offsets: int32 [7, 3], replicated, may hold values from -1 to 1, as said below
- branch: int32 [3], replicated, may hold values from 0 to 1, as said below
Outputs:
- new_density: float32 [16, 16, 7, 2, 128, 128], P('row', 'col')
- grad_density: float32 [16, 16, 7, 2, 128, 128], P('row', 'col')
- totals: float32 [2], replicated
The draws below stay inside these ranges and needn't reach their ends.
Inputs may be any that keep to these rules, and one draw needn't show every extreme that they name: 7 distinct offsets; (0, 0, 0) is one of them and with each offset its negative (layer step modulo 2) is another; row and column steps lie in -1 to 1, and nonzero row steps and nonzero column steps both occur. `branch`: each entry is 0 or 1, and not all entries are equal. `density`: the matrix is symmetric: entry [p, q, t, s] is the transpose of the entry of the opposite offset at the transposed block position. `hamiltonian`: the matrix is symmetric, in the same sense as the density.
All inputs are finite; a program needn't handle non-finite values.
Results may differ from the reference program's by a relative error of at most 0.0003.
Values sent between devices are 32-bit elements; how exact they have to be, the bound alone decides.
A program may use at most 128 MiB of HBM per device.

```python
import jax
import jax.numpy as jnp
from jax import lax

BLOCK = 128
LAYERS = 2
SLOTS = 7
STEPS = 3
ORDER = 65536
N_ROW = 16
N_COL = 16


def offset_table(key):
    candidates = jnp.array([[1, -1, 0], [1, -1, 1], [1, 0, 0], [1, 0, 1], [1, 1, 0], [1, 1, 1], [0, 1, 0], [0, 1, 1]], jnp.int32)
    picked = jax.random.permutation(jax.random.fold_in(key, 11), 8)
    chosen = candidates[picked[:3]]
    negated = jnp.stack([-chosen[:, 0], -chosen[:, 1], (LAYERS - chosen[:, 2]) % LAYERS], axis=1)
    offset_rows = jnp.concatenate([jnp.zeros((1, 3), jnp.int32), chosen, negated], axis=0)
    shuffle = jax.random.permutation(jax.random.fold_in(key, 12), SLOTS)
    return offset_rows[shuffle]


def zero_mask(key):
    return jnp.all(offset_table(key) == 0, axis=1).astype(jnp.float32)


def draw_offsets(key, part):
    return offset_table(key)


def draw_branch(key, part):
    number = jax.random.randint(jax.random.fold_in(key, 41), (), 1, 2 ** STEPS - 1, jnp.int32)
    powers = 2 ** jnp.arange(STEPS, dtype=jnp.int32)
    return (number // powers % 2).astype(jnp.int32)


def symmetric(raw_blocks, table):
    negated = jnp.stack([-table[:, 0], -table[:, 1], (LAYERS - table[:, 2]) % LAYERS], axis=1)
    matching = jnp.all(negated[:, None, :] == table[None, :, :], axis=-1).astype(jnp.int32)
    opposite = jnp.argmax(matching, axis=1).astype(jnp.int32)
    mirrored_list = []
    for slot in range(SLOTS):
        other = jnp.take(raw_blocks, opposite[slot], axis=2)
        other = jnp.roll(other, -table[slot, 0], axis=0)
        other = jnp.roll(other, table[slot, 1], axis=1)
        other = jnp.roll(other, -table[slot, 2], axis=2)
        mirrored_list.append(jnp.swapaxes(other, -1, -2))
    mirrored = jnp.stack(mirrored_list, axis=2)
    return (raw_blocks + mirrored) * 0.5 ** 0.5


def rough_part(noise_key, shape):
    return jax.random.truncated_normal(noise_key, -4.0, 4.0, shape, jnp.float32)


def draw_density(key, part):
    shape = (N_ROW, N_COL, SLOTS, LAYERS, BLOCK, BLOCK)
    table = offset_table(key)
    zero_slot = zero_mask(key)
    noise_key = jax.random.fold_in(key, 21)
    rough_key = jax.random.fold_in(key, 23)
    noise_part = symmetric(rough_part(noise_key, shape), table) * (0.5 / (BLOCK * SLOTS) ** 0.5)
    levels = 0.25 + 0.5 * lax.iota(jnp.float32, N_ROW) / (N_ROW - 1)
    roughness = jax.random.uniform(rough_key, (N_ROW, N_COL, SLOTS, LAYERS, BLOCK), jnp.float32, 0.6, 1.4)
    diagonal_part = levels[:, None, None, None, None] * roughness * zero_slot[None, None, :, None, None]
    unit_block = jnp.eye(BLOCK, dtype=jnp.float32)
    return noise_part + diagonal_part[..., None] * unit_block


def draw_hamiltonian(key, part):
    shape = (N_ROW, N_COL, SLOTS, LAYERS, BLOCK, BLOCK)
    table = offset_table(key)
    zero_slot = zero_mask(key)
    noise_key = jax.random.fold_in(key, 31)
    onsite_key = jax.random.fold_in(key, 33)
    hopping = symmetric(rough_part(noise_key, shape), table) * 0.3
    onsite = jax.random.uniform(onsite_key, (N_ROW, N_COL, SLOTS, LAYERS, BLOCK), jnp.float32, 0.5, 2.0)
    onsite = onsite * zero_slot[None, None, :, None, None]
    unit_block = jnp.eye(BLOCK, dtype=jnp.float32)
    return hopping + onsite[..., None] * unit_block


def setup_inputs(seed: int = 0) -> dict:
    key_of = jax.random.split(jax.random.key(seed), 5)
    density = draw_density(jax.random.fold_in(key_of[4], 71), 0)
    hamiltonian = draw_hamiltonian(jax.random.fold_in(key_of[4], 71), 0)
    offsets = draw_offsets(jax.random.fold_in(key_of[4], 71), 0)
    branch = draw_branch(jax.random.fold_in(key_of[4], 71), 0)
    return dict(density=density, hamiltonian=hamiltonian, offsets=offsets, branch=branch)


FULL_PRECISION = lax.Precision.HIGHEST


def pair_tables(offsets, row_count, col_count, layer_count):
    moduli = jnp.array([row_count, col_count, layer_count], jnp.int32)
    summed = offsets[:, None, :] + offsets[None, :, :]
    differ = summed[None, :, :, :] - offsets[:, None, None, :]
    matches = jnp.all(differ % moduli == 0, axis=-1).astype(jnp.int32)
    partner = jnp.argmax(matches, axis=2).astype(jnp.int32)
    usable = jnp.max(matches, axis=2)
    return partner, usable


def sparse_product(left, right, offsets, partner, usable):
    count_offsets = offsets.shape[0]

    def pair_step(pair_index, running):
        target = (pair_index // count_offsets).astype(jnp.int32)
        left_index = (pair_index % count_offsets).astype(jnp.int32)
        partner_slot = partner[target, left_index]
        left_part = lax.dynamic_index_in_dim(left, left_index, 2, keepdims=False)
        left_part = jnp.roll(left_part, offsets[partner_slot, 1], axis=1)
        right_part = lax.dynamic_index_in_dim(right, partner_slot, 2, keepdims=False)
        right_part = jnp.roll(right_part, -offsets[left_index, 0], axis=0)
        right_part = jnp.roll(right_part, -offsets[left_index, 2], axis=2)
        block_term = jnp.einsum('pqsab,pqsbc->pqsac', left_part, right_part, precision=FULL_PRECISION)
        keep_mask = usable[target, left_index].astype(block_term.dtype)
        current = lax.dynamic_index_in_dim(running, target, 2, keepdims=False)
        return lax.dynamic_update_index_in_dim(running, current + keep_mask * block_term, target, 2)

    return lax.fori_loop(0, count_offsets * count_offsets, pair_step, jnp.zeros_like(left))


def reference(density, hamiltonian, offsets, branch):
    partner, usable = pair_tables(offsets, N_ROW, N_COL, LAYERS)
    zero_slot = jnp.all(offsets == 0, axis=1).astype(jnp.float32)
    identity_part = zero_slot[:, None, None, None] * jnp.eye(BLOCK, dtype=jnp.float32)
    branch_signs = (2 * branch - 1).astype(jnp.float32)
    iterates = [density]
    for step in range(STEPS):
        current = iterates[-1]
        square = sparse_product(current, current, offsets, partner, usable)
        iterates.append(current + branch_signs[step] * (current - square))
    new_density = iterates[-1]
    energy = jnp.sum(hamiltonian * new_density) / ORDER
    occupation = jnp.sum(new_density * identity_part) / ORDER
    totals = jnp.stack([energy, occupation])
    outer_grad = hamiltonian + (occupation - 0.5) * identity_part
    for step in range(STEPS - 1, -1, -1):
        current = iterates[step]
        cross = sparse_product(outer_grad, current, offsets, partner, usable) + sparse_product(current, outer_grad, offsets, partner, usable)
        outer_grad = (1.0 + branch_signs[step]) * outer_grad - branch_signs[step] * cross
    return (new_density, outer_grad, totals)
```

```python
import functools

import jax
import jax.numpy as jnp
from jax import lax
from jax.experimental import pallas as pl
from jax.experimental.pallas import tpu as pltpu
from jax.sharding import PartitionSpec as P

ROW, COL = "row", "col"
MESH_ID = pl.DeviceIdType.MESH
F32, BF16, I32 = jnp.float32, jnp.bfloat16, jnp.int32
B = 128

X0, X1, X2, HAM, G2, G1, X3, G0 = range(8)


def split(value):
    high = value.astype(BF16)
    return high, (value - high.astype(F32)).astype(BF16)


def fold(r):
    return (r[:B, :B] + r[B:, B:]) + (r[:B, B:] + r[B:, :B])


def dot(a, b, dims):
    return lax.dot_general(a, b, (dims, ((), ())), preferred_element_type=F32)


def cat(parts, axis):
    return jnp.concatenate(parts, axis=axis)


def dot_nn(lefts, rights):
    lhs = cat([cat([h for h, _ in lefts], 1), cat([l for _, l in lefts], 1)], 0)
    rhs = cat([cat([h, l], 1) for h, l in rights], 0)
    return fold(dot(lhs, rhs, ((1,), (0,))))


def dot_tn(left, right):
    return fold(dot(cat(left, 1), cat(right, 1), ((0,), (0,))))


def dot_nt(left, right):
    return fold(dot(cat(left, 0), cat(right, 0), ((1,), (1,))))


def gram(high, low):
    return dot(high, cat([high, low], 1), ((0,), (0,)))


def total(conditions, values):
    return functools.reduce(lambda a, b: a + b, [jnp.where(c, v, 0) for c, v in zip(conditions, values)])


def kernel(
    eta, n_row, n_col, order,
    off_ref, branch_ref, x_hbm, h_hbm,
    new_hbm, grad_hbm, tot_ref,
    raw_x, raw_h, cf, eh, el, dh, dl, rd, sp, rp, ow, ox, rx, ar_src, ar, out_new, out_grad, tab,
    in_sem, out_sem, d_send, d_recv, p_send, p_recv, x_send, x_recv, ar_send, ar_recv,
):
    p, q = lax.axis_index(ROW), lax.axis_index(COL)
    up, down = lax.rem(p + 1, n_row), lax.rem(p + n_row - 1, n_row)
    right, left = lax.rem(q + 1, n_col), lax.rem(q + n_col - 1, n_col)

    loads = [
        pltpu.make_async_copy(x_hbm.at[0, 0], raw_x, in_sem.at[0]),
        pltpu.make_async_copy(h_hbm.at[0, 0], raw_h, in_sem.at[1]),
    ]
    for load in loads:
        load.start()

    barrier = pltpu.get_barrier_semaphore()

    def greet_row(d, carry):
        pl.semaphore_signal(barrier, inc=1, device_id=(lax.rem(p + d, n_row), q), device_id_type=MESH_ID)
        return carry

    def greet_col(d, carry):
        pl.semaphore_signal(barrier, inc=1, device_id=(p, lax.rem(q + d, n_col)), device_id_type=MESH_ID)
        return carry

    lax.fori_loop(1, n_row, greet_row, 0)
    lax.fori_loop(1, n_col, greet_col, 0)
    greeted = n_row + n_col - 2
    if eta:
        corners = [(up, left if eta > 0 else right), (down, right if eta > 0 else left)]
        for corner in corners:
            pl.semaphore_signal(barrier, inc=1, device_id=corner, device_id_type=MESH_ID)
        greeted += 2

    off = [[off_ref[t, c] for c in range(3)] for t in range(7)]
    lay = [lax.rem(o[2] + 2, 2) for o in off]
    zero = [(o[0] == 0) & (o[1] == 0) & (s == 0) for o, s in zip(off, lay)]
    slots = [total(zero, range(7))]
    steps = [(0, 0, 0)]
    if eta:
        firsts = [[(o[0] == a) & (o[1] == b) for o in off] for a, b in ((1, 0), (0, eta), (1, eta))]
    else:
        lead = [(o[0] == 1) | ((o[0] == 0) & (o[1] == 1)) for o in off]
        before, count = [], jnp.int32(0)
        for is_lead in lead:
            before.append(count)
            count = count + jnp.where(is_lead, 1, 0)
        firsts = [[is_lead & (b == j) for is_lead, b in zip(lead, before)] for j in range(3)]
    for first in firsts:
        a, b, s = total(first, [o[0] for o in off]), total(first, [o[1] for o in off]), total(first, lay)
        mirror = [(o[0] == -a) & (o[1] == -b) & (t == s) for o, t in zip(off, lay)]
        slots += [total(first, range(7)), total(mirror, range(7))]
        steps += [(a, b, s), (-a, -b, s)]
    for k in range(7):
        tab[0, k] = jnp.clip(slots[k], 0, 6)
        for c in range(3):
            tab[1 + c, k] = jnp.clip(jnp.int32(0) + steps[k][c], -1, 1)
    for t in range(7):
        tab[4, t] = jnp.clip(total([slots[k] == t for k in range(7)], range(7)), 0, 6)
    signs = [(2 * branch_ref[k] - 1).astype(F32) for k in range(3)]
    keep = [jnp.where(steps[1 + 2 * j][0] != 0, 1.0, 0.0).astype(F32) for j in range(3)]

    def take_in(which, x):
        loads[which].wait()
        raw = (raw_x, raw_h)[which]

        def body(k, carry):
            slot = tab[0, k]
            cf[x, k] = raw[slot]
            return carry

        lax.fori_loop(0, 7, body, 0)

    def split_edges(x):
        def body(i, carry):
            for s in range(2):
                eh[x, i, s], el[x, i, s] = split(cf[x, i + 1, s])
            return carry

        lax.fori_loop(0, 6, body, 0)

    def split_diagonal(x):
        for s in range(2):
            high, low = split(cf[x, 0, s])
            for place in (1, 4):
                dh[x, place, s], dl[x, place, s] = high, low

    def diagonal_copies(x):
        targets = ((p, right), (p, left), (up, q), (down, q))
        return [
            pltpu.make_async_remote_copy(
                src_ref=cf.at[x, 0],
                dst_ref=rd.at[x, i],
                send_sem=d_send.at[x, i],
                recv_sem=d_recv.at[x, i],
                device_id=target,
                device_id_type=MESH_ID,
            )
            for i, target in enumerate(targets)
        ]

    def send_diagonal(x):
        for copy in diagonal_copies(x):
            copy.start()

    def receive_diagonal(x):
        for i, copy in enumerate(diagonal_copies(x)):
            copy.wait_recv()
            for s in range(2):
                place = (0, 2, 3, 5)[i]
                dh[x, place, s], dl[x, place, s] = split(rd[x, i, s])

    def partial_copies(n):
        return [
            pltpu.make_async_remote_copy(
                src_ref=sp.at[n, g],
                dst_ref=rp.at[n, g],
                send_sem=p_send.at[n, g],
                recv_sem=p_recv.at[n, g],
                device_id=((up, q), (down, q))[g],
                device_id_type=MESH_ID,
            )
            for g in range(2)
        ]

    def corner_copies(n):
        copies = []
        for j in range(3):
            for g in range(2):
                row_to = (up, down)[g]
                col_to = (left, right)[g] if eta > 0 else (right, left)[g]
                target = ((row_to, q), (p, col_to), (row_to, col_to))[j]
                copies.append(
                    pltpu.make_async_remote_copy(
                        src_ref=ox.at[n, j, g],
                        dst_ref=rx[n].at[j, 1 - g],
                        send_sem=x_send.at[n, 2 * j + g],
                        recv_sem=x_recv.at[n, 2 * j + g],
                        device_id=target,
                        device_id_type=MESH_ID,
                    )
                )
        return copies

    def edge(x, k, s):
        return eh[x, k - 1, s], el[x, k - 1, s]

    def send_partials(n, x, g=None):
        def body(s, carry):
            own = None
            for sign in range(2):
                sent = None
                for j in range(3):
                    k = 1 + 2 * j + sign
                    source = lax.rem(s + tab[3, k], 2)
                    if g is None:
                        r = gram(*edge(x, k, source))
                    else:
                        r = dot_tn(edge(g, k, source), edge(x, k, source))
                    away = r * keep[j]
                    stay = r - away
                    sent = away if sent is None else sent + away
                    own = stay if own is None else own + stay
                if g is None:
                    sp[n, sign, s] = sent[:, :B] + sent[:, B:] + sent[:, B:].T
                else:
                    sp[n, sign, s] = sent + sent.T
            if g is None:
                own = own + gram(dh[x, 1, s], dl[x, 1, s])
                ow[n, s] = own[:, :B] + own[:, B:] + own[:, B:].T
            else:
                own = own + dot_nn([(dh[g, 1, s], dl[g, 1, s])], [(dh[x, 1, s], dl[x, 1, s])])
                ow[n, s] = own + own.T
            return carry

        lax.fori_loop(0, 2, body, 0)
        for copy in partial_copies(n):
            copy.start()
        if not eta:
            return

        def corners_body(i, carry):
            sign, s = i // 2, lax.rem(i, 2)
            other = lax.rem(s + steps[3][2], 2)
            pairs = [(x, x)] if g is None else [(g, x), (x, g)]
            ka, kb, kc = 1 + sign, 3 + sign, 5 + sign
            ox[n, 0, sign, s] = functools.reduce(
                jnp.add, [dot_tn(edge(u, kb, s), edge(v, kc, s)) for u, v in pairs]
            )
            ox[n, 1, sign, s] = functools.reduce(
                jnp.add, [dot_nt(edge(u, kc, s), edge(v, ka, other)) for u, v in pairs]
            )
            ox[n, 2, sign, s] = functools.reduce(
                jnp.add, [dot_nn([edge(u, kb, s)], [edge(v, ka, other)]) for u, v in pairs]
            )
            return carry

        lax.fori_loop(0, 4, corners_body, 0)
        for copy in corner_copies(n):
            copy.start()

    def update_edges(n, sign, x, out, g=None, excess=None):
        base = x if g is None else g
        if eta:
            for copy in corner_copies(n):
                copy.wait_recv()
        lb = steps[3][2]
        lc = steps[5][2]

        def body(i, carry):
            k = i + 1
            to_left, to_right = 1 - tab[2, k], 4 + tab[1, k]
            for s in range(2):
                t = lax.rem(s + tab[3, k], 2)

                def near(m):
                    return (dh[m, to_left, s], dl[m, to_left, s]), (dh[m, to_right, t], dl[m, to_right, t])

                x_left, x_right = near(x)
                x_edge = (eh[x, i, s], el[x, i, s])
                if g is None:
                    product = dot_nn([x_left, x_edge], [x_edge, x_right])
                else:
                    g_left, g_right = near(g)
                    g_edge = (eh[g, i, s], el[g, i, s])
                    product = dot_nn([g_left, x_left, g_edge, x_edge], [x_edge, g_edge, x_right, g_right])
                if eta:
                    j, sg = i // 2, lax.rem(i, 2)
                    mine = jnp.where(j == 0, lb, 0)
                    theirs = jnp.where(j == 1, lb, lc)
                    product = product + ox[n, j, sg, lax.rem(s + mine, 2)] + rx[n][j, sg, lax.rem(s + theirs, 2)].T
                value = (1.0 + sign) * cf[base, k, s] - sign * product
                if excess is not None:
                    value = value - (2.0 * sign * excess) * cf[x, k, s]
                cf[out, k, s] = value
                if out < X3:
                    eh[out, i, s], el[out, i, s] = split(value)
            return carry

        lax.fori_loop(0, 6, body, 0)

    eye = lax.broadcasted_iota(I32, (B, B), 0) == lax.broadcasted_iota(I32, (B, B), 1)

    def update_diagonal(n, sign, x, out, g=None, excess=None):
        base = x if g is None else g
        for copy in partial_copies(n):
            copy.wait_recv()
        for s in range(2):
            product = ow[n, s] + rp[n, 0, s] + rp[n, 1, s]
            value = (1.0 + sign) * cf[base, 0, s] - sign * product
            if excess is not None:
                value = value + jnp.where(eye, (1.0 + sign) * excess, 0.0) - (2.0 * sign * excess) * cf[x, 0, s]
            cf[out, 0, s] = value
        if out < X3:
            split_diagonal(out)
            send_diagonal(out)

    def reduce_copy(turn, stage, d):
        return pltpu.make_async_remote_copy(
            src_ref=ar_src.at[turn, stage],
            dst_ref=ar.at[turn, stage, d],
            send_sem=ar_send.at[turn, stage, d],
            recv_sem=ar_recv.at[turn, stage, d],
            device_id=(lax.rem(p + d, n_row), q) if stage == 0 else (p, lax.rem(q + d, n_col)),
            device_id_type=MESH_ID,
        )

    def reduce_start(turn, stage, value):
        ar_src[turn, stage] = value

        def body(d, carry):
            reduce_copy(turn, stage, d).start()
            return carry

        lax.fori_loop(1, (n_row, n_col)[stage], body, 0)

    def reduce_end(turn, stage):
        count = (n_row, n_col)[stage]

        def wait(d, carry):
            reduce_copy(turn, stage, d).wait_recv()
            return carry

        lax.fori_loop(1, count, wait, 0)
        return lax.fori_loop(1, count, lambda d, v: v + ar[turn, stage, d], ar_src[turn, stage])

    def tiles(value):
        return jnp.sum(value.reshape(-1, 8, B), axis=0)

    def trace_of(x):
        return functools.reduce(jnp.add, [tiles(jnp.where(eye, cf[x, 0, s], 0.0)) for s in range(2)])

    def dot_all(a, b):
        def body(k, carry):
            return carry + tiles(cf[a, k] * cf[b, k])

        return lax.fori_loop(0, 7, body, jnp.zeros((8, B), F32))

    def put_out(x, which, hbm):
        out_buf = (out_new, out_grad)[which]
        def body(t, carry):
            slot = tab[4, t]
            out_buf[t] = cf[x, slot]
            return carry

        lax.fori_loop(0, 7, body, 0)
        copy = pltpu.make_async_copy(out_buf, hbm.at[0, 0], out_sem.at[which])
        copy.start()
        return copy

    take_in(0, X0)
    pl.semaphore_wait(barrier, greeted)
    send_diagonal(X0)
    split_edges(X0)
    split_diagonal(X0)
    send_partials(0, X0)
    take_in(1, HAM)
    send_diagonal(HAM)
    split_edges(HAM)
    split_diagonal(HAM)
    for n in range(2):
        if n:
            send_partials(n, n)
        update_diagonal(n, signs[n], n, n + 1)
        receive_diagonal(n)
        update_edges(n, signs[n], n, n + 1)
    last = signs[2]
    send_partials(3, X2, HAM)
    occupied = (1.0 + last) * trace_of(X2) - last * dot_all(X2, X2)
    reduce_start(0, 0, jnp.stack([occupied, occupied]))
    send_partials(2, X2)
    reduce_start(0, 1, reduce_end(0, 0))
    receive_diagonal(HAM)
    receive_diagonal(X2)
    excess = jnp.sum(reduce_end(0, 1)[0]) / order - 0.5
    update_diagonal(3, last, X2, G2, HAM, excess)
    update_edges(3, last, X2, G2, HAM, excess)
    send_partials(4, X1, G2)
    update_diagonal(2, last, X2, X3)
    update_edges(2, last, X2, X3)
    reduce_start(1, 0, jnp.stack([dot_all(HAM, X3), trace_of(X3)]))
    first_out = put_out(X3, 0, new_hbm)
    update_diagonal(4, signs[1], X1, G1, G2)
    receive_diagonal(G2)
    update_edges(4, signs[1], X1, G1, G2)
    send_partials(5, X0, G1)
    reduce_start(1, 1, reduce_end(1, 0))
    update_diagonal(5, signs[0], X0, G0, G1)
    receive_diagonal(G1)
    update_edges(5, signs[0], X0, G0, G1)
    second_out = put_out(G0, 1, grad_hbm)
    sums = reduce_end(1, 1)
    tot_ref[0] = jnp.sum(sums[0]) / order
    tot_ref[1] = jnp.sum(sums[1]) / order

    for x in range(6):
        for copy in diagonal_copies(x) + partial_copies(x) + (corner_copies(x) if eta else []):
            copy.wait_send()
    for turn in range(2):
        for stage in range(2):

            def wait(d, carry):
                reduce_copy(turn, stage, d).wait_send()
                return carry

            lax.fori_loop(1, (n_row, n_col)[stage], wait, 0)
    first_out.wait()
    second_out.wait()


def call(eta, n_row, n_col, density, hamiltonian, offsets, branch):
    blocks = density.shape[2:]
    order = float(n_row * n_col * blocks[1] * blocks[2])
    extra = 6 if eta else 1
    any_space = pl.BlockSpec(memory_space=pl.ANY)
    smem = pl.BlockSpec(memory_space=pltpu.SMEM)
    dma = pltpu.SemaphoreType.DMA
    width = max(n_row, n_col)
    return pl.pallas_call(
        functools.partial(kernel, eta, n_row, n_col, order),
        out_shape=(
            jax.ShapeDtypeStruct(density.shape, F32),
            jax.ShapeDtypeStruct(density.shape, F32),
            jax.ShapeDtypeStruct((2,), F32),
        ),
        in_specs=[smem, smem, any_space, any_space],
        out_specs=(any_space, any_space, smem),
        scratch_shapes=[
            pltpu.VMEM((7, 2, B, B), F32),
            pltpu.VMEM((7, 2, B, B), F32),
            pltpu.VMEM((8, 7, 2, B, B), F32),
            pltpu.VMEM((6, 6, 2, B, B), BF16),
            pltpu.VMEM((6, 6, 2, B, B), BF16),
            pltpu.VMEM((6, 6, 2, B, B), BF16),
            pltpu.VMEM((6, 6, 2, B, B), BF16),
            pltpu.VMEM((6, 4, 2, B, B), F32),
            pltpu.VMEM((6, 2, 2, B, B), F32),
            pltpu.VMEM((6, 2, 2, B, B), F32),
            pltpu.VMEM((6, 2, B, B), F32),
            pltpu.VMEM((extra, 3, 2, 2, B, B), F32),
            [pltpu.VMEM((3, 2, 2, B, B), F32)] * extra,
            pltpu.VMEM((2, 2, 2, 8, B), F32),
            pltpu.VMEM((2, 2, width, 2, 8, B), F32),
            pltpu.VMEM((7, 2, B, B), F32),
            pltpu.VMEM((7, 2, B, B), F32),
            pltpu.SMEM((5, 8), I32),
            dma((2,)),
            dma((2,)),
            dma((6, 4)),
            dma((6, 4)),
            dma((6, 2)),
            dma((6, 2)),
            dma((6, 6)),
            dma((6, 6)),
            dma((2, 2, width)),
            dma((2, 2, width)),
        ],
        compiler_params=pltpu.CompilerParams(
            collective_id=1 + eta, has_side_effects=True, vmem_limit_bytes=56 * 1024 * 1024
        ),
        name="sp2_" + ("mirrored", "open", "closed")[1 + eta],
    )(offsets, branch, density, hamiltonian)


def pattern_class(offsets):
    rows, cols = offsets[:, 0], offsets[:, 1]
    layers = offsets[:, 2] % 2

    def find(a, b):
        here = (rows == a) & (cols == b)
        return jnp.any(here), jnp.sum(jnp.where(here, layers, 0))

    has_a, layer_a = find(1, 0)
    has_b, layer_b = find(0, 1)
    has_c, layer_c = find(1, 1)
    has_d, layer_d = find(1, -1)
    pair = has_a & has_b
    plus = pair & has_c & ((layer_a + layer_b + layer_c) % 2 == 0)
    minus = pair & has_d & ((layer_a + layer_b + layer_d) % 2 == 0)
    return jnp.where(plus, 1, jnp.where(minus, 2, 0)).astype(I32)


def solution(mesh):
    n_row, n_col = mesh.shape[ROW], mesh.shape[COL]

    def local(density, hamiltonian, offsets, branch):
        branches = [functools.partial(call, eta, n_row, n_col) for eta in (0, 1, -1)]
        return lax.switch(pattern_class(offsets), branches, density, hamiltonian, offsets, branch)

    spec = P(ROW, COL, None, None, None, None)
    return jax.shard_map(
        local, mesh=mesh, in_specs=(spec, spec, P(), P()), out_specs=(spec, spec, P()), check_vma=False
    )
```

```python
import functools

import jax
import jax.numpy as jnp
from jax import lax
from jax.experimental import pallas as pl
from jax.experimental.pallas import tpu as pltpu
from jax.sharding import PartitionSpec as P

ROW, COL = "row", "col"
MESH_ID = pl.DeviceIdType.MESH
F32, BF16, I32 = jnp.float32, jnp.bfloat16, jnp.int32
B = 128
PACKED = B + 8

X0, X1, X2, HAM, G2, G1, X3, G0 = range(8)


def split(value):
    high = value.astype(BF16)
    return high, (value - high.astype(F32)).astype(BF16)


def fold(r):
    return (r[:B, :B] + r[B:, B:]) + (r[:B, B:] + r[B:, :B])


def dot(a, b, dims):
    return lax.dot_general(a, b, (dims, ((), ())), preferred_element_type=F32)


def cat(parts, axis):
    return jnp.concatenate(parts, axis=axis)


def dot_nn(lefts, rights):
    lhs = cat([cat([h for h, _ in lefts], 1), cat([l for _, l in lefts], 1)], 0)
    rhs = cat([cat([h, l], 1) for h, l in rights], 0)
    return fold(dot(lhs, rhs, ((1,), (0,))))


def dot_tn(left, right):
    return fold(dot(cat(left, 1), cat(right, 1), ((0,), (0,))))


def dot_nt(left, right):
    return fold(dot(cat(left, 0), cat(right, 0), ((1,), (1,))))


def gram(high, low):
    return dot(high, cat([high, low], 1), ((0,), (0,)))


def total(conditions, values):
    return functools.reduce(lambda a, b: a + b, [jnp.where(c, v, 0) for c, v in zip(conditions, values)])


def kernel(
    eta, n_row, n_col, order,
    off_ref, branch_ref, x_hbm, h_hbm,
    new_ref, grad_ref, tot_ref,
    raw_x, raw_h, cf, eh, el, dh, dl, sd, rd, parts, sp, rp, ow, ox, rx, ar_src, ar, tab,
    in_sem, d_send, d_recv, p_send, p_recv, x_send, x_recv, ar_send, ar_recv,
):
    p, q = lax.axis_index(ROW), lax.axis_index(COL)
    up, down = lax.rem(p + 1, n_row), lax.rem(p + n_row - 1, n_row)
    right, left = lax.rem(q + 1, n_col), lax.rem(q + n_col - 1, n_col)

    row_id = lax.broadcasted_iota(I32, (B, B), 0)
    col_id = lax.broadcasted_iota(I32, (B, B), 1)
    eye, lower = row_id == col_id, row_id >= col_id

    def pack(ref, first, second):
        ref[0:B, :] = jnp.where(lower, first, second)
        ref[B : B + 1, :] = jnp.sum(jnp.where(eye, second, 0.0), axis=0, keepdims=True)

    def unpack(both, diagonal):
        flipped = both.T
        second = jnp.where(lower, flipped, both)
        return jnp.where(lower, both, flipped), jnp.where(eye, diagonal, second)

    loads = [
        pltpu.make_async_copy(x_hbm.at[0, 0], raw_x, in_sem.at[0]),
        pltpu.make_async_copy(h_hbm.at[0, 0], raw_h, in_sem.at[1]),
    ]
    for load in loads:
        load.start()

    barrier = pltpu.get_barrier_semaphore()

    def greet_row(d, carry):
        pl.semaphore_signal(barrier, inc=1, device_id=(lax.rem(p + d, n_row), q), device_id_type=MESH_ID)
        return carry

    def greet_col(d, carry):
        pl.semaphore_signal(barrier, inc=1, device_id=(p, lax.rem(q + d, n_col)), device_id_type=MESH_ID)
        return carry

    lax.fori_loop(1, n_row, greet_row, 0)
    lax.fori_loop(1, n_col, greet_col, 0)
    greeted = n_row + n_col - 2
    if eta:
        corners = [(up, left if eta > 0 else right), (down, right if eta > 0 else left)]
        for corner in corners:
            pl.semaphore_signal(barrier, inc=1, device_id=corner, device_id_type=MESH_ID)
        greeted += 2

    off = [[off_ref[t, c] for c in range(3)] for t in range(7)]
    lay = [lax.rem(o[2] + 2, 2) for o in off]
    zero = [(o[0] == 0) & (o[1] == 0) & (s == 0) for o, s in zip(off, lay)]
    slots = [total(zero, range(7))]
    steps = [(0, 0, 0)]
    if eta:
        firsts = [[(o[0] == a) & (o[1] == b) for o in off] for a, b in ((1, 0), (0, eta), (1, eta))]
    else:
        lead = [(o[0] == 1) | ((o[0] == 0) & (o[1] == 1)) for o in off]
        before, count = [], jnp.int32(0)
        for is_lead in lead:
            before.append(count)
            count = count + jnp.where(is_lead, 1, 0)
        firsts = [[is_lead & (b == j) for is_lead, b in zip(lead, before)] for j in range(3)]
    for first in firsts:
        a, b, s = total(first, [o[0] for o in off]), total(first, [o[1] for o in off]), total(first, lay)
        mirror = [(o[0] == -a) & (o[1] == -b) & (t == s) for o, t in zip(off, lay)]
        slots += [total(first, range(7)), total(mirror, range(7))]
        steps += [(a, b, s), (-a, -b, s)]
    for k in range(7):
        tab[0, k] = jnp.clip(slots[k], 0, 6)
        for c in range(3):
            tab[1 + c, k] = jnp.clip(jnp.int32(0) + steps[k][c], -1, 1)
    for t in range(7):
        tab[4, t] = jnp.clip(total([slots[k] == t for k in range(7)], range(7)), 0, 6)
    signs = [(2 * branch_ref[k] - 1).astype(F32) for k in range(3)]
    keep = [jnp.where(steps[1 + 2 * j][0] != 0, 1.0, 0.0).astype(F32) for j in range(3)]

    def take_in(which, x):
        loads[which].wait()
        raw = (raw_x, raw_h)[which]

        def body(k, carry):
            slot = tab[0, k]
            cf[x, k] = raw[slot]
            return carry

        lax.fori_loop(0, 7, body, 0)

    def split_edges(x):
        def body(i, carry):
            for s in range(2):
                eh[x, i, s], el[x, i, s] = split(cf[x, i + 1, s])
            return carry

        lax.fori_loop(0, 6, body, 0)

    def split_diagonal(x):
        for s in range(2):
            high, low = split(cf[x, 0, s])
            for place in (1, 4):
                dh[x, place, s], dl[x, place, s] = high, low

    def diagonal_copies(x):
        targets = ((p, right), (p, left), (up, q), (down, q))
        return [
            pltpu.make_async_remote_copy(
                src_ref=sd.at[x],
                dst_ref=rd.at[x, i],
                send_sem=d_send.at[x, i],
                recv_sem=d_recv.at[x, i],
                device_id=target,
                device_id_type=MESH_ID,
            )
            for i, target in enumerate(targets)
        ]

    def send_diagonal(x):
        pack(sd.at[x], cf[x, 0, 0], cf[x, 0, 1])
        for copy in diagonal_copies(x):
            copy.start()

    def receive_diagonal(x, extra=None):
        for i, copy in enumerate(diagonal_copies(x)):
            copy.wait_recv()
            place = (0, 2, 3, 5)[i]
            for s, value in enumerate(unpack(rd[x, i, 0:B, :], rd[x, i, B : B + 1, :])):
                if extra is not None:
                    value = value + extra(dh[X2, place, s].astype(F32) + dl[X2, place, s].astype(F32))
                dh[x, place, s], dl[x, place, s] = split(value)

    def partial_copies(n):
        return [
            pltpu.make_async_remote_copy(
                src_ref=sp.at[n, g],
                dst_ref=rp.at[n, g],
                send_sem=p_send.at[n, g],
                recv_sem=p_recv.at[n, g],
                device_id=((up, q), (down, q))[g],
                device_id_type=MESH_ID,
            )
            for g in range(2)
        ]

    def corner_copies(n):
        copies = []
        for j in range(3):
            for g in range(2):
                row_to = (up, down)[g]
                col_to = (left, right)[g] if eta > 0 else (right, left)[g]
                target = ((row_to, q), (p, col_to), (row_to, col_to))[j]
                copies.append(
                    pltpu.make_async_remote_copy(
                        src_ref=ox.at[n, j, g],
                        dst_ref=rx[n].at[j, 1 - g],
                        send_sem=x_send.at[n, 2 * j + g],
                        recv_sem=x_recv.at[n, 2 * j + g],
                        device_id=target,
                        device_id_type=MESH_ID,
                    )
                )
        return copies

    def edge(x, k, s):
        return eh[x, k - 1, s], el[x, k - 1, s]

    def send_partials(n, x, g=None):
        def body(s, carry):
            own = None
            for sign in range(2):
                sent = None
                for j in range(3):
                    k = 1 + 2 * j + sign
                    source = lax.rem(s + tab[3, k], 2)
                    if g is None:
                        r = gram(*edge(x, k, source))
                    else:
                        r = dot_tn(edge(g, k, source), edge(x, k, source))
                    away = r * keep[j]
                    stay = r - away
                    sent = away if sent is None else sent + away
                    own = stay if own is None else own + stay
                if g is None:
                    parts[sign, s] = sent[:, :B] + sent[:, B:] + sent[:, B:].T
                else:
                    parts[sign, s] = sent + sent.T
            if g is None:
                own = own + gram(dh[x, 1, s], dl[x, 1, s])
                ow[n, s] = own[:, :B] + own[:, B:] + own[:, B:].T
            else:
                own = own + dot_nn([(dh[g, 1, s], dl[g, 1, s])], [(dh[x, 1, s], dl[x, 1, s])])
                ow[n, s] = own + own.T
            return carry

        lax.fori_loop(0, 2, body, 0)
        for sign, copy in enumerate(partial_copies(n)):
            pack(sp.at[n, sign], parts[sign, 0], parts[sign, 1])
            copy.start()
        if not eta:
            return

        def corners_body(i, carry):
            sign, s = i // 2, lax.rem(i, 2)
            other = lax.rem(s + steps[3][2], 2)
            pairs = [(x, x)] if g is None else [(g, x), (x, g)]
            ka, kb, kc = 1 + sign, 3 + sign, 5 + sign
            ox[n, 0, sign, s] = functools.reduce(
                jnp.add, [dot_tn(edge(u, kb, s), edge(v, kc, s)) for u, v in pairs]
            )
            ox[n, 1, sign, s] = functools.reduce(
                jnp.add, [dot_nt(edge(u, kc, s), edge(v, ka, other)) for u, v in pairs]
            )
            ox[n, 2, sign, s] = functools.reduce(
                jnp.add, [dot_nn([edge(u, kb, s)], [edge(v, ka, other)]) for u, v in pairs]
            )
            return carry

        lax.fori_loop(0, 4, corners_body, 0)
        for copy in corner_copies(n):
            copy.start()

    def update_edges(n, sign, x, out, g=None, extra=None):
        base = x if g is None else g
        if eta:
            for copy in corner_copies(n) + (corner_copies(6) if extra is not None else []):
                copy.wait_recv()
        lb = steps[3][2]
        lc = steps[5][2]

        def body(i, carry):
            k = i + 1
            to_left, to_right = 1 - tab[2, k], 4 + tab[1, k]
            for s in range(2):
                t = lax.rem(s + tab[3, k], 2)

                def near(m):
                    return (dh[m, to_left, s], dl[m, to_left, s]), (dh[m, to_right, t], dl[m, to_right, t])

                x_left, x_right = near(x)
                x_edge = (eh[x, i, s], el[x, i, s])
                if g is None:
                    product = dot_nn([x_left, x_edge], [x_edge, x_right])
                else:
                    g_left, g_right = near(g)
                    g_edge = (eh[g, i, s], el[g, i, s])
                    product = dot_nn([g_left, x_left, g_edge, x_edge], [x_edge, g_edge, x_right, g_right])
                if eta:
                    j, sg = i // 2, lax.rem(i, 2)
                    mine = jnp.where(j == 0, lb, 0)
                    theirs = jnp.where(j == 1, lb, lc)
                    corner = ox[n, j, sg, lax.rem(s + mine, 2)] + rx[n][j, sg, lax.rem(s + theirs, 2)].T
                    product = product + corner
                    if extra is not None:
                        corner = ox[6, j, sg, lax.rem(s + mine, 2)] + rx[6][j, sg, lax.rem(s + theirs, 2)].T
                        product = product + extra * corner
                value = (1.0 + sign) * cf[base, k, s] - sign * product
                cf[out, k, s] = value
                if out < X3:
                    eh[out, i, s], el[out, i, s] = split(value)
            return carry

        lax.fori_loop(0, 6, body, 0)

    def update_diagonal(n, sign, x, out, g=None, extra=None):
        base = x if g is None else g
        for copy in partial_copies(n) + (partial_copies(6) if extra is not None else []):
            copy.wait_recv()
        arrived = rp[n, 0] + rp[n, 1]
        if extra is not None:
            one, same = extra
            arrived = arrived + same * (rp[6, 0] + rp[6, 1])
        for s, product in enumerate(unpack(arrived[0:B, :], arrived[B : B + 1, :])):
            product = product + ow[n, s]
            if extra is not None:
                product = product + same * ow[6, s] + (2.0 * one) * cf[x, 0, s]
            cf[out, 0, s] = (1.0 + sign) * cf[base, 0, s] - sign * product
        if out < X3:
            split_diagonal(out)
            send_diagonal(out)

    def reduce_copy(turn, stage, d):
        return pltpu.make_async_remote_copy(
            src_ref=ar_src.at[turn, stage],
            dst_ref=ar.at[turn, stage, d],
            send_sem=ar_send.at[turn, stage, d],
            recv_sem=ar_recv.at[turn, stage, d],
            device_id=(lax.rem(p + d, n_row), q) if stage == 0 else (p, lax.rem(q + d, n_col)),
            device_id_type=MESH_ID,
        )

    def reduce_start(turn, stage, value):
        ar_src[turn, stage] = value

        def body(d, carry):
            reduce_copy(turn, stage, d).start()
            return carry

        lax.fori_loop(1, (n_row, n_col)[stage], body, 0)

    def reduce_end(turn, stage):
        count = (n_row, n_col)[stage]

        def wait(d, carry):
            reduce_copy(turn, stage, d).wait_recv()
            return carry

        lax.fori_loop(1, count, wait, 0)
        return lax.fori_loop(1, count, lambda d, v: v + ar[turn, stage, d], ar_src[turn, stage])

    def tiles(value):
        return jnp.sum(value.reshape(-1, 8, B), axis=0)

    def trace_of(x):
        return functools.reduce(jnp.add, [tiles(jnp.where(eye, cf[x, 0, s], 0.0)) for s in range(2)])

    def dot_all(a, b):
        def body(k, carry):
            return carry + tiles(cf[a, k] * cf[b, k])

        return lax.fori_loop(0, 7, body, jnp.zeros((8, B), F32))

    def put_out(x, ref):
        def body(t, carry):
            slot = tab[4, t]
            ref[0, 0, t] = cf[x, slot]
            return carry

        lax.fori_loop(0, 7, body, 0)

    take_in(0, X0)
    pl.semaphore_wait(barrier, greeted)
    send_diagonal(X0)
    split_edges(X0)
    split_diagonal(X0)
    send_partials(0, X0)
    take_in(1, HAM)
    split_edges(HAM)
    split_diagonal(HAM)
    update_diagonal(0, signs[0], X0, X1)
    receive_diagonal(X0)
    update_edges(0, signs[0], X0, X1)
    send_partials(1, X1)
    send_diagonal(HAM)
    update_diagonal(1, signs[1], X1, X2)
    receive_diagonal(X1)
    update_edges(1, signs[1], X1, X2)
    last = signs[2]
    send_partials(3, X2, HAM)
    occupied = (1.0 + last) * trace_of(X2) - last * dot_all(X2, X2)
    reduce_start(0, 0, jnp.stack([occupied, occupied]))
    send_partials(6, X1, X2)
    reduce_start(0, 1, reduce_end(0, 0))
    update_diagonal(3, last, X2, G2, HAM)
    receive_diagonal(HAM)
    receive_diagonal(X2)
    update_edges(3, last, X2, G2, HAM)
    send_partials(4, X1, G2)
    send_partials(2, X2)
    excess = jnp.sum(reduce_end(0, 1)[0]) / order - 0.5
    one, same = (1.0 + last) * excess, -2.0 * last * excess

    def complete(k, carry):
        for s in range(2):
            value = cf[G2, k, s] + same * cf[X2, k, s]
            cf[G2, k, s] = value
            eh[G2, k - 1, s], el[G2, k - 1, s] = split(value)
        return carry

    lax.fori_loop(1, 7, complete, 0)
    for s in range(2):
        cf[G2, 0, s] = cf[G2, 0, s] + jnp.where(eye, one, 0.0) + same * cf[X2, 0, s]
    split_diagonal(G2)
    update_diagonal(4, signs[1], X1, G1, G2, (one, same))
    receive_diagonal(G2, lambda value: jnp.where(eye, one, 0.0) + same * value)
    update_edges(4, signs[1], X1, G1, G2, same)
    send_partials(5, X0, G1)
    update_edges(2, last, X2, X3)
    update_diagonal(2, last, X2, X3)
    reduce_start(1, 0, jnp.stack([dot_all(HAM, X3), trace_of(X3)]))
    update_diagonal(5, signs[0], X0, G0, G1)
    put_out(X3, new_ref)
    reduce_start(1, 1, reduce_end(1, 0))
    receive_diagonal(G1)
    update_edges(5, signs[0], X0, G0, G1)
    put_out(G0, grad_ref)
    sums = reduce_end(1, 1)
    tot_ref[0] = jnp.sum(sums[0]) / order
    tot_ref[1] = jnp.sum(sums[1]) / order

    for x in range(6):
        for copy in diagonal_copies(x):
            copy.wait_send()
    for n in range(7):
        for copy in partial_copies(n) + (corner_copies(n) if eta else []):
            copy.wait_send()
    for turn in range(2):
        for stage in range(2):

            def wait(d, carry):
                reduce_copy(turn, stage, d).wait_send()
                return carry

            lax.fori_loop(1, (n_row, n_col)[stage], wait, 0)


def call(eta, n_row, n_col, density, hamiltonian, offsets, branch):
    blocks = density.shape[2:]
    order = float(n_row * n_col * blocks[1] * blocks[2])
    extra = 7 if eta else 1
    any_space = pl.BlockSpec(memory_space=pl.ANY)
    vmem = pl.BlockSpec(memory_space=pltpu.VMEM)
    smem = pl.BlockSpec(memory_space=pltpu.SMEM)
    dma = pltpu.SemaphoreType.DMA
    width = max(n_row, n_col)
    return pl.pallas_call(
        functools.partial(kernel, eta, n_row, n_col, order),
        out_shape=(
            jax.ShapeDtypeStruct(density.shape, F32),
            jax.ShapeDtypeStruct(density.shape, F32),
            jax.ShapeDtypeStruct((2,), F32),
        ),
        in_specs=[smem, smem, any_space, any_space],
        out_specs=(vmem, vmem, smem),
        scratch_shapes=[
            pltpu.VMEM((7, 2, B, B), F32),
            pltpu.VMEM((7, 2, B, B), F32),
            pltpu.VMEM((8, 7, 2, B, B), F32),
            pltpu.VMEM((6, 6, 2, B, B), BF16),
            pltpu.VMEM((6, 6, 2, B, B), BF16),
            pltpu.VMEM((6, 6, 2, B, B), BF16),
            pltpu.VMEM((6, 6, 2, B, B), BF16),
            pltpu.VMEM((6, PACKED, B), F32),
            pltpu.VMEM((6, 4, PACKED, B), F32),
            pltpu.VMEM((2, 2, B, B), F32),
            pltpu.VMEM((7, 2, PACKED, B), F32),
            pltpu.VMEM((7, 2, PACKED, B), F32),
            pltpu.VMEM((7, 2, B, B), F32),
            pltpu.VMEM((extra, 3, 2, 2, B, B), F32),
            [pltpu.VMEM((3, 2, 2, B, B), F32)] * extra,
            pltpu.VMEM((2, 2, 2, 8, B), F32),
            pltpu.VMEM((2, 2, width, 2, 8, B), F32),
            pltpu.SMEM((5, 8), I32),
            dma((2,)),
            dma((6, 4)),
            dma((6, 4)),
            dma((7, 2)),
            dma((7, 2)),
            dma((7, 6)),
            dma((7, 6)),
            dma((2, 2, width)),
            dma((2, 2, width)),
        ],
        compiler_params=pltpu.CompilerParams(
            collective_id=1 + eta, has_side_effects=True, vmem_limit_bytes=56 * 1024 * 1024
        ),
        name="sp2_" + ("mirrored", "open", "closed")[1 + eta],
    )(offsets, branch, density, hamiltonian)


def pattern_class(offsets):
    rows, cols, layers = offsets[:, 0], offsets[:, 1], offsets[:, 2] & 1
    kind = jnp.where(rows == 1, jnp.where(cols == 0, 1, jnp.where(cols == 1, 64, 512)), 8)
    leads = (rows == 1) | ((rows == 0) & (cols == 1))
    code = jnp.sum(jnp.where(leads, kind + (layers << 12), 0))
    seen, even = code & 4095, (code & 4096) == 0
    return jnp.where(even & (seen == 73), 1, jnp.where(even & (seen == 521), 2, 0)).astype(I32)


def solution(mesh):
    n_row, n_col = mesh.shape[ROW], mesh.shape[COL]

    def local(density, hamiltonian, offsets, branch):
        branches = [functools.partial(call, eta, n_row, n_col) for eta in (0, 1, -1)]
        return lax.switch(pattern_class(offsets), branches, density, hamiltonian, offsets, branch)

    spec = P(ROW, COL, None, None, None, None)
    return jax.shard_map(
        local, mesh=mesh, in_specs=(spec, spec, P(), P()), out_specs=(spec, spec, P()), check_vma=False
    )
```

```python
import functools

import jax
import jax.numpy as jnp
from jax import lax
from jax.experimental import pallas as pl
from jax.experimental.pallas import tpu as pltpu
from jax.sharding import PartitionSpec as P

ROW, COL = "row", "col"
MESH_ID = pl.DeviceIdType.MESH
F32, BF16, I32 = jnp.float32, jnp.bfloat16, jnp.int32
B = 128
PACKED = B + 8

X0, X1, X2, HAM, G2, G1, X3, G0 = range(8)


def split(value):
    high = value.astype(BF16)
    return high, (value - high.astype(F32)).astype(BF16)


def fold(r):
    return (r[:B, :B] + r[B:, B:]) + (r[:B, B:] + r[B:, :B])


def dot(a, b, dims):
    return lax.dot_general(a, b, (dims, ((), ())), preferred_element_type=F32)


def cat(parts, axis):
    return jnp.concatenate(parts, axis=axis)


def dot_nn(lefts, rights):
    lhs = cat([cat([h for h, _ in lefts], 1), cat([l for _, l in lefts], 1)], 0)
    rhs = cat([cat([h, l], 1) for h, l in rights], 0)
    return fold(dot(lhs, rhs, ((1,), (0,))))


def dot_tn(left, right):
    return fold(dot(cat(left, 1), cat(right, 1), ((0,), (0,))))


def dot_nt(left, right):
    return fold(dot(cat(left, 0), cat(right, 0), ((1,), (1,))))


def gram(high, low):
    return dot(high, cat([high, low], 1), ((0,), (0,)))


def total(conditions, values):
    return functools.reduce(lambda a, b: a + b, [jnp.where(c, v, 0) for c, v in zip(conditions, values)])


def kernel(
    eta, n_row, n_col, order,
    off_ref, branch_ref, x_hbm, h_hbm,
    new_ref, grad_ref, tot_ref,
    raw_x, raw_h, cf, eh, el, dh, dl, sd, rd, parts, sp, rp, ow, ox, st, sa, ra, ah, al, ext, rv, rt, ar_src, ar, tab,
    in_sem, d_send, d_recv, p_send, p_recv, x_send, x_recv, ar_send, ar_recv,
):
    p, q = lax.axis_index(ROW), lax.axis_index(COL)
    up, down = lax.rem(p + 1, n_row), lax.rem(p + n_row - 1, n_row)
    right, left = lax.rem(q + 1, n_col), lax.rem(q + n_col - 1, n_col)

    row_id = lax.broadcasted_iota(I32, (B, B), 0)
    col_id = lax.broadcasted_iota(I32, (B, B), 1)
    eye, lower = row_id == col_id, row_id >= col_id

    def pack(ref, first, second):
        ref[0:B, :] = jnp.where(lower, first, second)
        ref[B : B + 1, :] = jnp.sum(jnp.where(eye, second, 0.0), axis=0, keepdims=True)

    def unpack(both, diagonal):
        flipped = both.T
        second = jnp.where(lower, flipped, both)
        return jnp.where(lower, both, flipped), jnp.where(eye, diagonal, second)

    loads = [
        pltpu.make_async_copy(x_hbm.at[0, 0], raw_x, in_sem.at[0]),
        pltpu.make_async_copy(h_hbm.at[0, 0], raw_h, in_sem.at[1]),
    ]
    for load in loads:
        load.start()

    barrier = pltpu.get_barrier_semaphore()

    def greet_row(d, carry):
        pl.semaphore_signal(barrier, inc=1, device_id=(lax.rem(p + d, n_row), q), device_id_type=MESH_ID)
        return carry

    def greet_col(d, carry):
        pl.semaphore_signal(barrier, inc=1, device_id=(p, lax.rem(q + d, n_col)), device_id_type=MESH_ID)
        return carry

    lax.fori_loop(1, n_row, greet_row, 0)
    lax.fori_loop(1, n_col, greet_col, 0)
    greeted = n_row + n_col - 2
    off = [[off_ref[c, t] for c in range(3)] for t in range(7)]
    lay = [lax.rem(o[2] + 2, 2) for o in off]
    zero = [(o[0] == 0) & (o[1] == 0) & (s == 0) for o, s in zip(off, lay)]
    slots = [total(zero, range(7))]
    steps = [(0, 0, 0)]
    if eta:
        firsts = [[(o[0] == a) & (o[1] == b) for o in off] for a, b in ((1, 0), (0, eta), (1, eta))]
    else:
        lead = [(o[0] == 1) | ((o[0] == 0) & (o[1] == 1)) for o in off]
        before, count = [], jnp.int32(0)
        for is_lead in lead:
            before.append(count)
            count = count + jnp.where(is_lead, 1, 0)
        firsts = [[is_lead & (b == j) for is_lead, b in zip(lead, before)] for j in range(3)]
    for first in firsts:
        a, b, s = total(first, [o[0] for o in off]), total(first, [o[1] for o in off]), total(first, lay)
        mirror = [(o[0] == -a) & (o[1] == -b) & (t == s) for o, t in zip(off, lay)]
        slots += [total(first, range(7)), total(mirror, range(7))]
        steps += [(a, b, s), (-a, -b, s)]
    for k in range(7):
        tab[0, k] = jnp.clip(slots[k], 0, 6)
        for c in range(3):
            tab[1 + c, k] = jnp.clip(jnp.int32(0) + steps[k][c], -1, 1)
    for t in range(7):
        tab[4, t] = jnp.clip(total([slots[k] == t for k in range(7)], range(7)), 0, 6)
    signs = [(2 * branch_ref[k] - 1).astype(F32) for k in range(3)]
    keep = [jnp.where(steps[1 + 2 * j][0] != 0, 1.0, 0.0).astype(F32) for j in range(3)]

    def take_in(which, x):
        loads[which].wait()
        raw = (raw_x, raw_h)[which]

        def body(k, carry):
            slot = tab[0, k]
            cf[x, k] = raw[slot]
            return carry

        lax.fori_loop(0, 7, body, 0)

    def split_edges(x):
        def body(i, carry):
            for s in range(2):
                eh[x, i, s], el[x, i, s] = split(cf[x, i + 1, s])
            return carry

        lax.fori_loop(0, 6, body, 0)

    def split_diagonal(x):
        for s in range(2):
            high, low = split(cf[x, 0, s])
            for place in (1, 4):
                dh[x, place, s], dl[x, place, s] = high, low

    def diagonal_copies(x):
        targets = ((p, right), (p, left), (up, q), (down, q))
        return [
            pltpu.make_async_remote_copy(
                src_ref=sd.at[x],
                dst_ref=rd.at[x, i],
                send_sem=d_send.at[x, i],
                recv_sem=d_recv.at[x, i],
                device_id=target,
                device_id_type=MESH_ID,
            )
            for i, target in enumerate(targets)
        ]

    def send_diagonal(x):
        pack(sd.at[x], cf[x, 0, 0], cf[x, 0, 1])
        for copy in diagonal_copies(x):
            copy.start()

    def receive_diagonal(x, extra=None):
        for i, copy in enumerate(diagonal_copies(x)):
            copy.wait_recv()
            place = (0, 2, 3, 5)[i]
            for s, value in enumerate(unpack(rd[x, i, 0:B, :], rd[x, i, B : B + 1, :])):
                if extra is not None:
                    value = value + extra(dh[X2, place, s].astype(F32) + dl[X2, place, s].astype(F32))
                dh[x, place, s], dl[x, place, s] = split(value)

    def partial_copies(n):
        return [
            pltpu.make_async_remote_copy(
                src_ref=sp.at[n, g],
                dst_ref=rp.at[n, g],
                send_sem=p_send.at[n, g],
                recv_sem=p_recv.at[n, g],
                device_id=((up, q), (down, q))[g],
                device_id_type=MESH_ID,
            )
            for g in range(2)
        ]

    toward = ((left, right) if eta > 0 else (right, left)) if eta else None

    def corner_copy(src, dst, x, i, target):
        return pltpu.make_async_remote_copy(
            src_ref=src,
            dst_ref=dst,
            send_sem=x_send.at[x, i],
            recv_sem=x_recv.at[x, i],
            device_id=target,
            device_id_type=MESH_ID,
        )

    def operand_copies(x):
        targets = ((p, toward[0]), (p, toward[1]), (up, q), (down, q))
        return [corner_copy(sa.at[x, i], ra.at[x, i], x, i, target) for i, target in enumerate(targets)]

    def first_copies(n):
        return [corner_copy(ox.at[n, 0, g], rv[n].at[1 - g], n, 4 + g, ((up, q), (down, q))[g]) for g in range(2)]

    def second_copies(n):
        return [corner_copy(st.at[n, g], rt[n].at[1 - g], n, 6 + g, ((up, q), (down, q))[g]) for g in range(2)]

    def corner_all(n):
        return operand_copies(n) + first_copies(n) + second_copies(n) if eta else []

    def send_operands(x):
        if not eta:
            return
        for i, copy in enumerate(operand_copies(x)):
            sa[x, i] = cf[x, (1, 2, 5, 6)[i]]
            copy.start()

    def receive_operands(x, same=None):
        if not eta:
            return
        for copy in operand_copies(x):
            copy.wait_recv()

        def body(i, carry):
            for s in range(2):
                value = ra[x, i, s]
                if same is not None:
                    value = value + same * (ah[X2, i, s].astype(F32) + al[X2, i, s].astype(F32))
                ah[x, i, s], al[x, i, s] = split(value)
            return carry

        lax.fori_loop(0, 4, body, 0)

    def summed(terms):
        return functools.reduce(jnp.add, terms)

    def send_corners(n, x, g=None):
        if not eta:
            return
        pairs = [(x, x)] if g is None else [(g, x), (x, g)]

        def body(i, carry):
            sign, s = i // 2, lax.rem(i, 2)
            other = lax.rem(s + steps[3][2], 2)
            ka, kb, kc = 1 + sign, 3 + sign, 5 + sign
            ox[n, 0, sign, s] = summed([dot_tn(edge(u, kb, s), edge(v, kc, s)) for u, v in pairs])
            ox[n, 1, sign, s] = summed([dot_nt(edge(u, kc, s), edge(v, ka, other)) for u, v in pairs])
            ox[n, 2, sign, s] = summed([dot_nn([edge(u, kb, s)], [edge(v, ka, other)]) for u, v in pairs])
            return carry

        lax.fori_loop(0, 4, body, 0)
        for copy in first_copies(n):
            copy.start()

    def send_seconds(n, x, g=None):
        if not eta:
            return
        pairs = [(x, x)] if g is None else [(g, x), (x, g)]

        def operand(m, i, s):
            return ah[m, i, s], al[m, i, s]

        def body(i, carry):
            sign, s = i // 2, lax.rem(i, 2)
            st[n, sign, s] = summed([dot_tn(edge(u, 4 - sign, s), operand(v, sign, s)) for u, v in pairs])
            return carry

        lax.fori_loop(0, 4, body, 0)
        for copy in second_copies(n):
            copy.start()

        def rest(i, carry):
            sign, s = i // 2, lax.rem(i, 2)
            other = lax.rem(s + steps[1][2], 2)
            ext[3 - sign, s] = ox[n, 1, 1 - sign, s] + summed(
                [dot_nn([operand(u, sign, s)], [operand(v, 3 - sign, other)]) for u, v in pairs]
            )
            return carry

        lax.fori_loop(0, 4, rest, 0)

    def gather_corners(n):
        for copy in first_copies(n) + second_copies(n):
            copy.wait_recv()
        la, lb, lc = steps[1][2], steps[3][2], steps[5][2]

        def body(i, carry):
            sign, s = i // 2, lax.rem(i, 2)
            ext[sign, s] = ox[n, 0, sign, lax.rem(s + lb, 2)] + rv[n][sign, lax.rem(s + lc, 2)].T
            ext[4 + sign, s] = ox[n, 2, sign, s] + rt[n][sign, lax.rem(s + la, 2)].T
            return carry

        lax.fori_loop(0, 4, body, 0)

    def edge(x, k, s):
        return eh[x, k - 1, s], el[x, k - 1, s]

    def send_partials(n, x, g=None):
        def body(s, carry):
            own = None
            for sign in range(2):
                sent = None
                for j in range(3):
                    k = 1 + 2 * j + sign
                    source = lax.rem(s + tab[3, k], 2)
                    if g is None:
                        r = gram(*edge(x, k, source))
                    else:
                        r = dot_tn(edge(g, k, source), edge(x, k, source))
                    away = r * keep[j]
                    stay = r - away
                    sent = away if sent is None else sent + away
                    own = stay if own is None else own + stay
                if g is None:
                    parts[sign, s] = sent[:, :B] + sent[:, B:] + sent[:, B:].T
                else:
                    parts[sign, s] = sent + sent.T
            if g is None:
                own = own + gram(dh[x, 1, s], dl[x, 1, s])
                ow[n, s] = own[:, :B] + own[:, B:] + own[:, B:].T
            else:
                own = own + dot_nn([(dh[g, 1, s], dl[g, 1, s])], [(dh[x, 1, s], dl[x, 1, s])])
                ow[n, s] = own + own.T
            return carry

        lax.fori_loop(0, 2, body, 0)
        for sign, copy in enumerate(partial_copies(n)):
            pack(sp.at[n, sign], parts[sign, 0], parts[sign, 1])
            copy.start()

    def update_edges(n, sign, x, out, g=None):
        base = x if g is None else g
        if eta:
            gather_corners(n)

        def body(i, carry):
            k = i + 1
            to_left, to_right = 1 - tab[2, k], 4 + tab[1, k]
            for s in range(2):
                t = lax.rem(s + tab[3, k], 2)

                def near(m):
                    return (dh[m, to_left, s], dl[m, to_left, s]), (dh[m, to_right, t], dl[m, to_right, t])

                x_left, x_right = near(x)
                x_edge = (eh[x, i, s], el[x, i, s])
                if g is None:
                    product = dot_nn([x_left, x_edge], [x_edge, x_right])
                else:
                    g_left, g_right = near(g)
                    g_edge = (eh[g, i, s], el[g, i, s])
                    product = dot_nn([g_left, x_left, g_edge, x_edge], [x_edge, g_edge, x_right, g_right])
                if eta:
                    product = product + ext[i, s]
                value = (1.0 + sign) * cf[base, k, s] - sign * product
                cf[out, k, s] = value
                if out < X3:
                    eh[out, i, s], el[out, i, s] = split(value)
            return carry

        lax.fori_loop(0, 6, body, 0)

    def update_diagonal(n, sign, x, out, g=None, extra=None):
        base = x if g is None else g
        for copy in partial_copies(n) + (partial_copies(6) if extra is not None else []):
            copy.wait_recv()
        arrived = rp[n, 0] + rp[n, 1]
        if extra is not None:
            one, same = extra
            arrived = arrived + same * (rp[6, 0] + rp[6, 1])
        for s, product in enumerate(unpack(arrived[0:B, :], arrived[B : B + 1, :])):
            product = product + ow[n, s]
            if extra is not None:
                product = product + same * ow[6, s] + (2.0 * one) * cf[x, 0, s]
            cf[out, 0, s] = (1.0 + sign) * cf[base, 0, s] - sign * product
        if out < X3:
            split_diagonal(out)
            send_diagonal(out)

    def reduce_copy(turn, stage, d):
        return pltpu.make_async_remote_copy(
            src_ref=ar_src.at[turn, stage],
            dst_ref=ar.at[turn, stage, d],
            send_sem=ar_send.at[turn, stage, d],
            recv_sem=ar_recv.at[turn, stage, d],
            device_id=(lax.rem(p + d, n_row), q) if stage == 0 else (p, lax.rem(q + d, n_col)),
            device_id_type=MESH_ID,
        )

    def reduce_start(turn, stage, value):
        ar_src[turn, stage] = value

        def body(d, carry):
            reduce_copy(turn, stage, d).start()
            return carry

        lax.fori_loop(1, (n_row, n_col)[stage], body, 0)

    def reduce_end(turn, stage):
        count = (n_row, n_col)[stage]

        def wait(d, carry):
            reduce_copy(turn, stage, d).wait_recv()
            return carry

        lax.fori_loop(1, count, wait, 0)
        return lax.fori_loop(1, count, lambda d, v: v + ar[turn, stage, d], ar_src[turn, stage])

    def tiles(value):
        return jnp.sum(value.reshape(-1, 8, B), axis=0)

    def lanes(first, second):
        return cat([jnp.sum(v, axis=0, keepdims=True) for v in (first, second)], 0)

    def trace_of(x):
        return functools.reduce(jnp.add, [tiles(jnp.where(eye, cf[x, 0, s], 0.0)) for s in range(2)])

    def dot_all(a, b):
        def body(k, carry):
            return carry + tiles(cf[a, k] * cf[b, k])

        return lax.fori_loop(0, 7, body, jnp.zeros((8, B), F32))

    def put_out(x, ref):
        def body(t, carry):
            slot = tab[4, t]
            ref[0, 0, t] = cf[x, slot]
            return carry

        lax.fori_loop(0, 7, body, 0)

    take_in(0, X0)
    pl.semaphore_wait(barrier, greeted)
    send_diagonal(X0)
    send_operands(X0)
    split_edges(X0)
    split_diagonal(X0)
    send_partials(0, X0)
    send_corners(0, X0)
    take_in(1, HAM)
    split_edges(HAM)
    split_diagonal(HAM)
    update_diagonal(0, signs[0], X0, X1)
    receive_operands(X0)
    send_seconds(0, X0)
    receive_diagonal(X0)
    update_edges(0, signs[0], X0, X1)
    send_operands(X1)
    send_partials(1, X1)
    send_corners(1, X1)
    send_diagonal(HAM)
    send_operands(HAM)
    update_diagonal(1, signs[1], X1, X2)
    receive_operands(X1)
    send_seconds(1, X1)
    receive_diagonal(X1)
    update_edges(1, signs[1], X1, X2)
    send_operands(X2)
    last = signs[2]
    send_partials(3, X2, HAM)
    occupied = (1.0 + last) * trace_of(X2) - last * dot_all(X2, X2)
    reduce_start(0, 0, lanes(occupied, occupied))
    send_corners(3, X2, HAM)
    send_partials(6, X1, X2)
    reduce_start(0, 1, reduce_end(0, 0))
    update_diagonal(3, last, X2, G2, HAM)
    receive_operands(HAM)
    receive_operands(X2)
    send_seconds(3, X2, HAM)
    receive_diagonal(HAM)
    receive_diagonal(X2)
    update_edges(3, last, X2, G2, HAM)
    send_operands(G2)
    send_partials(4, X1, G2)
    send_partials(2, X2)
    excess = jnp.sum(reduce_end(0, 1)[0:1]) / order - 0.5
    one, same = (1.0 + last) * excess, -2.0 * last * excess

    def complete(k, carry):
        for s in range(2):
            value = cf[G2, k, s] + same * cf[X2, k, s]
            cf[G2, k, s] = value
            eh[G2, k - 1, s], el[G2, k - 1, s] = split(value)
        return carry

    lax.fori_loop(1, 7, complete, 0)
    for s in range(2):
        cf[G2, 0, s] = cf[G2, 0, s] + jnp.where(eye, one, 0.0) + same * cf[X2, 0, s]
    split_diagonal(G2)
    update_diagonal(4, signs[1], X1, G1, G2, (one, same))
    send_corners(4, X1, G2)
    receive_operands(G2, same)
    send_seconds(4, X1, G2)
    receive_diagonal(G2, lambda value: jnp.where(eye, one, 0.0) + same * value)
    update_edges(4, signs[1], X1, G1, G2)
    send_operands(G1)
    send_partials(5, X0, G1)
    send_corners(5, X0, G1)
    send_corners(2, X2)
    send_seconds(2, X2)
    update_edges(2, last, X2, X3)
    update_diagonal(2, last, X2, X3)
    reduce_start(1, 0, lanes(dot_all(HAM, X3), trace_of(X3)))
    update_diagonal(5, signs[0], X0, G0, G1)
    put_out(X3, new_ref)
    reduce_start(1, 1, reduce_end(1, 0))
    receive_operands(G1)
    send_seconds(5, X0, G1)
    receive_diagonal(G1)
    update_edges(5, signs[0], X0, G0, G1)
    put_out(G0, grad_ref)
    sums = reduce_end(1, 1)
    tot_ref[0] = jnp.sum(sums[0:1]) / order
    tot_ref[1] = jnp.sum(sums[1:2]) / order

    for x in range(6):
        for copy in diagonal_copies(x):
            copy.wait_send()
    for n in range(7):
        for copy in partial_copies(n) + (corner_all(n) if n < 6 else []):
            copy.wait_send()
    for turn in range(2):
        for stage in range(2):

            def wait(d, carry):
                reduce_copy(turn, stage, d).wait_send()
                return carry

            lax.fori_loop(1, (n_row, n_col)[stage], wait, 0)


def call(eta, n_row, n_col, density, hamiltonian, offsets, branch):
    blocks = density.shape[2:]
    order = float(n_row * n_col * blocks[1] * blocks[2])
    extra = 6 if eta else 1
    any_space = pl.BlockSpec(memory_space=pl.ANY)
    vmem = pl.BlockSpec(memory_space=pltpu.VMEM)
    smem = pl.BlockSpec(memory_space=pltpu.SMEM)
    dma = pltpu.SemaphoreType.DMA
    width = max(n_row, n_col)
    return pl.pallas_call(
        functools.partial(kernel, eta, n_row, n_col, order),
        out_shape=(
            jax.ShapeDtypeStruct(density.shape, F32),
            jax.ShapeDtypeStruct(density.shape, F32),
            jax.ShapeDtypeStruct((2,), F32),
        ),
        in_specs=[smem, smem, any_space, any_space],
        out_specs=(vmem, vmem, smem),
        scratch_shapes=[
            pltpu.VMEM((7, 2, B, B), F32),
            pltpu.VMEM((7, 2, B, B), F32),
            pltpu.VMEM((8, 7, 2, B, B), F32),
            pltpu.VMEM((6, 6, 2, B, B), BF16),
            pltpu.VMEM((6, 6, 2, B, B), BF16),
            pltpu.VMEM((6, 6, 2, B, B), BF16),
            pltpu.VMEM((6, 6, 2, B, B), BF16),
            pltpu.VMEM((6, PACKED, B), F32),
            pltpu.VMEM((6, 4, PACKED, B), F32),
            pltpu.VMEM((2, 2, B, B), F32),
            pltpu.VMEM((7, 2, PACKED, B), F32),
            pltpu.VMEM((7, 2, PACKED, B), F32),
            pltpu.VMEM((7, 2, B, B), F32),
            pltpu.VMEM((extra, 3, 2, 2, B, B), F32),
            pltpu.VMEM((extra, 2, 2, B, B), F32),
            pltpu.VMEM((extra, 4, 2, B, B), F32),
            pltpu.VMEM((extra, 4, 2, B, B), F32),
            pltpu.VMEM((extra, 4, 2, B, B), BF16),
            pltpu.VMEM((extra, 4, 2, B, B), BF16),
            pltpu.VMEM((6, 2, B, B), F32),
            [pltpu.VMEM((2, 2, B, B), F32)] * extra,
            [pltpu.VMEM((2, 2, B, B), F32)] * extra,
            pltpu.VMEM((2, 2, 2, B), F32),
            pltpu.VMEM((2, 2, width, 2, B), F32),
            pltpu.SMEM((5, 8), I32),
            dma((2,)),
            dma((6, 4)),
            dma((6, 4)),
            dma((7, 2)),
            dma((7, 2)),
            dma((6, 8)),
            dma((6, 8)),
            dma((2, 2, width)),
            dma((2, 2, width)),
        ],
        compiler_params=pltpu.CompilerParams(
            collective_id=1 + eta, has_side_effects=True, vmem_limit_bytes=56 * 1024 * 1024
        ),
        name="sp2_" + ("mirrored", "open", "closed")[1 + eta],
    )(offsets.T, branch, density, hamiltonian)


def pattern_class(offsets):
    rows, cols, layers = offsets[:, 0], offsets[:, 1], offsets[:, 2] & 1
    kind = jnp.where(rows == 1, jnp.where(cols == 0, 1, jnp.where(cols == 1, 64, 512)), 8)
    leads = (rows == 1) | ((rows == 0) & (cols == 1))
    code = jnp.sum(jnp.where(leads, kind + (layers << 12), 0))
    seen, even = code & 4095, (code & 4096) == 0
    return jnp.where(even & (seen == 73), 1, jnp.where(even & (seen == 521), 2, 0)).astype(I32)


def solution(mesh):
    n_row, n_col = mesh.shape[ROW], mesh.shape[COL]

    def local(density, hamiltonian, offsets, branch):
        branches = [functools.partial(call, eta, n_row, n_col) for eta in (0, 1, -1)]
        return lax.switch(pattern_class(offsets), branches, density, hamiltonian, offsets, branch)

    spec = P(ROW, COL, None, None, None, None)
    return jax.shard_map(
        local, mesh=mesh, in_specs=(spec, spec, P(), P()), out_specs=(spec, spec, P()), check_vma=False
    )
```

```python
import functools

import jax
import jax.numpy as jnp
from jax import lax
from jax.experimental import pallas as pl
from jax.experimental.pallas import tpu as pltpu
from jax.sharding import PartitionSpec as P

ROW, COL = "row", "col"
MESH_ID = pl.DeviceIdType.MESH
F32, BF16, I32 = jnp.float32, jnp.bfloat16, jnp.int32
B = 128
PACKED = B + 8

X0, X1, X2, HAM, G2, G1, X3, G0 = range(8)


def split(value):
    high = value.astype(BF16)
    return high, (value - high.astype(F32)).astype(BF16)


def fold(r):
    return (r[:B, :B] + r[B:, B:]) + (r[:B, B:] + r[B:, :B])


def dot(a, b, dims):
    return lax.dot_general(a, b, (dims, ((), ())), preferred_element_type=F32)


def cat(parts, axis):
    return jnp.concatenate(parts, axis=axis)


def dot_nn(lefts, rights):
    lhs = cat([cat([h for h, _ in lefts], 1), cat([l for _, l in lefts], 1)], 0)
    rhs = cat([cat([h, l], 1) for h, l in rights], 0)
    return fold(dot(lhs, rhs, ((1,), (0,))))


def dot_tn(left, right):
    return fold(dot(cat(left, 1), cat(right, 1), ((0,), (0,))))


def dot_nt(left, right):
    return fold(dot(cat(left, 0), cat(right, 0), ((1,), (1,))))


def gram(high, low):
    return dot(high, cat([high, low], 1), ((0,), (0,)))


def total(conditions, values):
    return functools.reduce(lambda a, b: a + b, [jnp.where(c, v, 0) for c, v in zip(conditions, values)])


def kernel(
    eta, n_row, n_col, order,
    off_ref, branch_ref, x_hbm, h_hbm,
    new_ref, grad_ref, tot_ref,
    raw_x, raw_h, cf, eh, el, dh, dl, sd, rd, parts, sp, rp, ow, ox, st, sa, ra, ah, al, ext, rv, rt, ar_src, ar, tab,
    in_sem, d_send, d_recv, p_send, p_recv, x_send, x_recv, ar_send, ar_recv,
):
    p, q = lax.axis_index(ROW), lax.axis_index(COL)
    up, down = lax.rem(p + 1, n_row), lax.rem(p + n_row - 1, n_row)
    right, left = lax.rem(q + 1, n_col), lax.rem(q + n_col - 1, n_col)

    row_id = lax.broadcasted_iota(I32, (B, B), 0)
    col_id = lax.broadcasted_iota(I32, (B, B), 1)
    eye, lower = row_id == col_id, row_id >= col_id

    def pack(ref, first, second):
        ref[0:B, :] = jnp.where(lower, first, second)
        ref[B : B + 1, :] = jnp.sum(jnp.where(eye, second, 0.0), axis=0, keepdims=True)

    def unpack(both, diagonal):
        flipped = both.T
        second = jnp.where(lower, flipped, both)
        return jnp.where(lower, both, flipped), jnp.where(eye, diagonal, second)

    loads = [
        pltpu.make_async_copy(x_hbm.at[0, 0], raw_x, in_sem.at[0]),
        pltpu.make_async_copy(h_hbm.at[0, 0], raw_h, in_sem.at[1]),
    ]
    for load in loads:
        load.start()

    barrier = pltpu.get_barrier_semaphore()

    def greet_row(d, carry):
        pl.semaphore_signal(barrier, inc=1, device_id=(lax.rem(p + d, n_row), q), device_id_type=MESH_ID)
        return carry

    def greet_col(d, carry):
        pl.semaphore_signal(barrier, inc=1, device_id=(p, lax.rem(q + d, n_col)), device_id_type=MESH_ID)
        return carry

    lax.fori_loop(1, n_row, greet_row, 0)
    lax.fori_loop(1, n_col, greet_col, 0)
    greeted = n_row + n_col - 2
    off = [[off_ref[c, t] for c in range(3)] for t in range(7)]
    lay = [lax.rem(o[2] + 2, 2) for o in off]
    zero = [(o[0] == 0) & (o[1] == 0) & (s == 0) for o, s in zip(off, lay)]
    slots = [total(zero, range(7))]
    steps = [(0, 0, 0)]
    if eta:
        firsts = [[(o[0] == a) & (o[1] == b) for o in off] for a, b in ((1, 0), (0, eta), (1, eta))]
    else:
        lead = [(o[0] == 1) | ((o[0] == 0) & (o[1] == 1)) for o in off]
        before, count = [], jnp.int32(0)
        for is_lead in lead:
            before.append(count)
            count = count + jnp.where(is_lead, 1, 0)
        firsts = [[is_lead & (b == j) for is_lead, b in zip(lead, before)] for j in range(3)]
    for first in firsts:
        a, b, s = total(first, [o[0] for o in off]), total(first, [o[1] for o in off]), total(first, lay)
        mirror = [(o[0] == -a) & (o[1] == -b) & (t == s) for o, t in zip(off, lay)]
        slots += [total(first, range(7)), total(mirror, range(7))]
        steps += [(a, b, s), (-a, -b, s)]
    for k in range(7):
        tab[0, k] = jnp.clip(slots[k], 0, 6)
        for c in range(3):
            tab[1 + c, k] = jnp.clip(jnp.int32(0) + steps[k][c], -1, 1)
    for t in range(7):
        tab[4, t] = jnp.clip(total([slots[k] == t for k in range(7)], range(7)), 0, 6)
    signs = [(2 * branch_ref[k] - 1).astype(F32) for k in range(3)]
    keep = [jnp.where(steps[1 + 2 * j][0] != 0, 1.0, 0.0).astype(F32) for j in range(3)]

    def take_in(which, x, first, last):
        if not first:
            loads[which].wait()
        raw = (raw_x, raw_h)[which]

        def body(k, carry):
            slot = tab[0, k]
            cf[x, k] = raw[slot]
            return carry

        lax.fori_loop(first, last, body, 0)

    def split_edges(x):
        def body(i, carry):
            for s in range(2):
                eh[x, i, s], el[x, i, s] = split(cf[x, i + 1, s])
            return carry

        lax.fori_loop(0, 6, body, 0)

    def split_diagonal(x):
        for s in range(2):
            high, low = split(cf[x, 0, s])
            for place in (1, 4):
                dh[x, place, s], dl[x, place, s] = high, low

    def diagonal_copy(x, i):
        return pltpu.make_async_remote_copy(
            src_ref=sd.at[x],
            dst_ref=rd.at[x, i],
            send_sem=d_send.at[x, i],
            recv_sem=d_recv.at[x, i],
            device_id=((p, right), (p, left), (up, q), (down, q))[i],
            device_id_type=MESH_ID,
        )

    def diagonal_copies(x):
        return [diagonal_copy(x, i) for i in range(4)]

    def send_diagonal(x):
        pack(sd.at[x], cf[x, 0, 0], cf[x, 0, 1])
        for copy in diagonal_copies(x):
            copy.start()

    def receive_diagonal(x, extra=None):
        for i in (2, 3, 0, 1):
            diagonal_copy(x, i).wait_recv()
            place = (0, 2, 3, 5)[i]
            for s, value in enumerate(unpack(rd[x, i, 0:B, :], rd[x, i, B : B + 1, :])):
                if extra is not None:
                    value = value + extra(dh[X2, place, s].astype(F32) + dl[X2, place, s].astype(F32))
                dh[x, place, s], dl[x, place, s] = split(value)

    def partial_copies(n):
        return [
            pltpu.make_async_remote_copy(
                src_ref=sp.at[n, g],
                dst_ref=rp.at[n, g],
                send_sem=p_send.at[n, g],
                recv_sem=p_recv.at[n, g],
                device_id=((up, q), (down, q))[g],
                device_id_type=MESH_ID,
            )
            for g in range(2)
        ]

    toward = ((left, right) if eta > 0 else (right, left)) if eta else None

    def corner_copy(src, dst, x, i, target):
        return pltpu.make_async_remote_copy(
            src_ref=src,
            dst_ref=dst,
            send_sem=x_send.at[x, i],
            recv_sem=x_recv.at[x, i],
            device_id=target,
            device_id_type=MESH_ID,
        )

    def operand_copies(x):
        targets = ((p, toward[0]), (p, toward[1]), (up, q), (down, q))
        return [corner_copy(sa.at[x, i], ra.at[x, i], x, i, target) for i, target in enumerate(targets)]

    def first_copies(n):
        return [corner_copy(ox.at[n, 0, g], rv[n].at[1 - g], n, 4 + g, ((up, q), (down, q))[g]) for g in range(2)]

    def second_copies(n):
        return [corner_copy(st.at[n, g], rt[n].at[1 - g], n, 6 + g, ((up, q), (down, q))[g]) for g in range(2)]

    def corner_all(n):
        return operand_copies(n) + first_copies(n) + second_copies(n) if eta else []

    def send_operands(x):
        if not eta:
            return
        for i, copy in enumerate(operand_copies(x)):
            sa[x, i] = cf[x, (1, 2, 5, 6)[i]]
            copy.start()

    def receive_operands(x, same=None):
        if not eta:
            return
        for copy in operand_copies(x):
            copy.wait_recv()

        def body(i, carry):
            for s in range(2):
                value = ra[x, i, s]
                if same is not None:
                    value = value + same * (ah[X2, i, s].astype(F32) + al[X2, i, s].astype(F32))
                ah[x, i, s], al[x, i, s] = split(value)
            return carry

        lax.fori_loop(0, 4, body, 0)

    def summed(terms):
        return functools.reduce(jnp.add, terms)

    def send_corners(n, x, g=None):
        if not eta:
            return
        pairs = [(x, x)] if g is None else [(g, x), (x, g)]

        def body(i, carry):
            sign, s = i // 2, lax.rem(i, 2)
            other = lax.rem(s + steps[3][2], 2)
            ka, kb, kc = 1 + sign, 3 + sign, 5 + sign
            ox[n, 0, sign, s] = summed([dot_tn(edge(u, kb, s), edge(v, kc, s)) for u, v in pairs])
            ox[n, 1, sign, s] = summed([dot_nt(edge(u, kc, s), edge(v, ka, other)) for u, v in pairs])
            ox[n, 2, sign, s] = summed([dot_nn([edge(u, kb, s)], [edge(v, ka, other)]) for u, v in pairs])
            return carry

        lax.fori_loop(0, 4, body, 0)
        for copy in first_copies(n):
            copy.start()

    def send_seconds(n, x, g=None):
        if not eta:
            return
        pairs = [(x, x)] if g is None else [(g, x), (x, g)]

        def operand(m, i, s):
            return ah[m, i, s], al[m, i, s]

        def body(i, carry):
            sign, s = i // 2, lax.rem(i, 2)
            st[n, sign, s] = summed([dot_tn(edge(u, 4 - sign, s), operand(v, sign, s)) for u, v in pairs])
            return carry

        lax.fori_loop(0, 4, body, 0)
        for copy in second_copies(n):
            copy.start()

        def rest(i, carry):
            sign, s = i // 2, lax.rem(i, 2)
            other = lax.rem(s + steps[1][2], 2)
            ext[3 - sign, s] = ox[n, 1, 1 - sign, s] + summed(
                [dot_nn([operand(u, sign, s)], [operand(v, 3 - sign, other)]) for u, v in pairs]
            )
            return carry

        lax.fori_loop(0, 4, rest, 0)

    def gather_corners(n):
        for copy in first_copies(n) + second_copies(n):
            copy.wait_recv()
        la, lb, lc = steps[1][2], steps[3][2], steps[5][2]

        def body(i, carry):
            sign, s = i // 2, lax.rem(i, 2)
            ext[sign, s] = ox[n, 0, sign, lax.rem(s + lb, 2)] + rv[n][sign, lax.rem(s + lc, 2)].T
            ext[4 + sign, s] = ox[n, 2, sign, s] + rt[n][sign, lax.rem(s + la, 2)].T
            return carry

        lax.fori_loop(0, 4, body, 0)

    def edge(x, k, s):
        return eh[x, k - 1, s], el[x, k - 1, s]

    def send_partials(n, x, g=None):
        def body(s, carry):
            own = None
            for sign in range(2):
                sent = None
                for j in range(3):
                    k = 1 + 2 * j + sign
                    source = lax.rem(s + tab[3, k], 2)
                    if g is None:
                        r = gram(*edge(x, k, source))
                    else:
                        r = dot_tn(edge(g, k, source), edge(x, k, source))
                    away = r * keep[j]
                    stay = r - away
                    sent = away if sent is None else sent + away
                    own = stay if own is None else own + stay
                if g is None:
                    parts[sign, s] = sent[:, :B] + sent[:, B:] + sent[:, B:].T
                else:
                    parts[sign, s] = sent + sent.T
            if g is None:
                own = own + gram(dh[x, 1, s], dl[x, 1, s])
                ow[n, s] = own[:, :B] + own[:, B:] + own[:, B:].T
            else:
                own = own + dot_nn([(dh[g, 1, s], dl[g, 1, s])], [(dh[x, 1, s], dl[x, 1, s])])
                ow[n, s] = own + own.T
            return carry

        lax.fori_loop(0, 2, body, 0)
        for sign, copy in enumerate(partial_copies(n)):
            pack(sp.at[n, sign], parts[sign, 0], parts[sign, 1])
            copy.start()

    def update_edges(n, sign, x, out, g=None):
        base = x if g is None else g
        if eta:
            gather_corners(n)

        def body(i, carry):
            k = i + 1
            to_left, to_right = 1 - tab[2, k], 4 + tab[1, k]
            for s in range(2):
                t = lax.rem(s + tab[3, k], 2)

                def near(m):
                    return (dh[m, to_left, s], dl[m, to_left, s]), (dh[m, to_right, t], dl[m, to_right, t])

                x_left, x_right = near(x)
                x_edge = (eh[x, i, s], el[x, i, s])
                if g is None:
                    product = dot_nn([x_left, x_edge], [x_edge, x_right])
                else:
                    g_left, g_right = near(g)
                    g_edge = (eh[g, i, s], el[g, i, s])
                    product = dot_nn([g_left, x_left, g_edge, x_edge], [x_edge, g_edge, x_right, g_right])
                if eta:
                    product = product + ext[i, s]
                value = (1.0 + sign) * cf[base, k, s] - sign * product
                cf[out, k, s] = value
                if out < X3:
                    eh[out, i, s], el[out, i, s] = split(value)
            return carry

        lax.fori_loop(0, 6, body, 0)

    def update_diagonal(n, sign, x, out, g=None, extra=None):
        base = x if g is None else g
        for copy in partial_copies(n) + (partial_copies(6) if extra is not None else []):
            copy.wait_recv()
        arrived = rp[n, 0] + rp[n, 1]
        if extra is not None:
            one, same = extra
            arrived = arrived + same * (rp[6, 0] + rp[6, 1])
        for s, product in enumerate(unpack(arrived[0:B, :], arrived[B : B + 1, :])):
            product = product + ow[n, s]
            if extra is not None:
                product = product + same * ow[6, s] + (2.0 * one) * cf[x, 0, s]
            cf[out, 0, s] = (1.0 + sign) * cf[base, 0, s] - sign * product
        if out < X3:
            split_diagonal(out)
            send_diagonal(out)

    def reduce_copy(turn, stage, d):
        return pltpu.make_async_remote_copy(
            src_ref=ar_src.at[turn, stage],
            dst_ref=ar.at[turn, stage, d],
            send_sem=ar_send.at[turn, stage, d],
            recv_sem=ar_recv.at[turn, stage, d],
            device_id=(lax.rem(p + d, n_row), q) if stage == 0 else (p, lax.rem(q + d, n_col)),
            device_id_type=MESH_ID,
        )

    def reduce_start(turn, stage, value):
        ar_src[turn, stage] = value

        def body(d, carry):
            reduce_copy(turn, stage, d).start()
            return carry

        lax.fori_loop(1, (n_row, n_col)[stage], body, 0)

    def reduce_end(turn, stage):
        count = (n_row, n_col)[stage]

        def wait(d, carry):
            reduce_copy(turn, stage, d).wait_recv()
            return carry

        lax.fori_loop(1, count, wait, 0)
        return lax.fori_loop(1, count, lambda d, v: v + ar[turn, stage, d], ar_src[turn, stage])

    def sent(turn, stage):
        def wait(d, carry):
            reduce_copy(turn, stage, d).wait_send()
            return carry

        lax.fori_loop(1, (n_row, n_col)[stage], wait, 0)

    def tiles(value):
        return jnp.sum(value.reshape(-1, 8, B), axis=0)

    def lanes(first, second):
        return cat([jnp.sum(v, axis=0, keepdims=True) for v in (first, second)], 0)

    def trace_of(x):
        return functools.reduce(jnp.add, [tiles(jnp.where(eye, cf[x, 0, s], 0.0)) for s in range(2)])

    def dot_all(a, b):
        def body(k, carry):
            return carry + tiles(cf[a, k] * cf[b, k])

        return lax.fori_loop(0, 7, body, jnp.zeros((8, B), F32))

    def put_out(x, ref):
        def body(t, carry):
            slot = tab[4, t]
            ref[0, 0, t] = cf[x, slot]
            return carry

        lax.fori_loop(0, 7, body, 0)

    take_in(0, X0, 0, 1)
    pl.semaphore_wait(barrier, greeted)
    send_diagonal(X0)
    take_in(0, X0, 1, 7)
    send_operands(X0)
    split_edges(X0)
    split_diagonal(X0)
    send_partials(0, X0)
    send_corners(0, X0)
    take_in(1, HAM, 0, 7)
    split_edges(HAM)
    split_diagonal(HAM)
    update_diagonal(0, signs[0], X0, X1)
    receive_operands(X0)
    send_seconds(0, X0)
    receive_diagonal(X0)
    update_edges(0, signs[0], X0, X1)
    send_operands(X1)
    send_partials(1, X1)
    send_corners(1, X1)
    send_diagonal(HAM)
    send_operands(HAM)
    update_diagonal(1, signs[1], X1, X2)
    receive_operands(X1)
    send_seconds(1, X1)
    receive_diagonal(X1)
    update_edges(1, signs[1], X1, X2)
    send_operands(X2)
    last = signs[2]
    send_partials(3, X2, HAM)
    occupied = (1.0 + last) * trace_of(X2) - last * dot_all(X2, X2)
    reduce_start(0, 0, lanes(occupied, occupied))
    send_corners(3, X2, HAM)
    send_partials(6, X1, X2)
    update_diagonal(3, last, X2, G2, HAM)
    reduce_start(0, 1, reduce_end(0, 0))
    receive_operands(HAM)
    receive_operands(X2)
    send_seconds(3, X2, HAM)
    receive_diagonal(HAM)
    receive_diagonal(X2)
    update_edges(3, last, X2, G2, HAM)
    send_operands(G2)
    send_partials(4, X1, G2)
    send_partials(2, X2)
    energy = 0.5 * ((1.0 + last) * dot_all(HAM, X2) + dot_all(X2, G2))
    reduce_start(1, 0, lanes(energy, energy))
    occupation = jnp.sum(reduce_end(0, 1)[0:1]) / order
    excess = occupation - 0.5
    one, same = (1.0 + last) * excess, -2.0 * last * excess

    def complete(k, carry):
        for s in range(2):
            value = cf[G2, k, s] + same * cf[X2, k, s]
            cf[G2, k, s] = value
            eh[G2, k - 1, s], el[G2, k - 1, s] = split(value)
        return carry

    lax.fori_loop(1, 7, complete, 0)
    for s in range(2):
        cf[G2, 0, s] = cf[G2, 0, s] + jnp.where(eye, one, 0.0) + same * cf[X2, 0, s]
    split_diagonal(G2)
    update_diagonal(4, signs[1], X1, G1, G2, (one, same))
    send_corners(4, X1, G2)
    receive_operands(G2, same)
    send_seconds(4, X1, G2)
    receive_diagonal(G2, lambda value: jnp.where(eye, one, 0.0) + same * value)
    update_edges(4, signs[1], X1, G1, G2)
    send_operands(G1)
    send_partials(5, X0, G1)
    send_corners(5, X0, G1)
    reduce_start(1, 1, reduce_end(1, 0))
    send_corners(2, X2)
    send_seconds(2, X2)
    update_edges(2, last, X2, X3)
    update_diagonal(2, last, X2, X3)
    put_out(X3, new_ref)
    update_diagonal(5, signs[0], X0, G0, G1)
    receive_operands(G1)
    send_seconds(5, X0, G1)
    for x in range(5):
        for copy in diagonal_copies(x):
            copy.wait_send()
    for n in range(7):
        for copy in partial_copies(n) + (corner_all(n) if n < 6 else []):
            copy.wait_send()
    for turn, stage in ((0, 0), (0, 1), (1, 0)):
        sent(turn, stage)
    receive_diagonal(G1)
    update_edges(5, signs[0], X0, G0, G1)
    put_out(G0, grad_ref)
    sums = reduce_end(1, 1)
    tot_ref[0] = jnp.sum(sums[0:1]) / order
    tot_ref[1] = occupation

    for copy in diagonal_copies(G1):
        copy.wait_send()
    sent(1, 1)


def call(eta, n_row, n_col, density, hamiltonian, offsets, branch):
    blocks = density.shape[2:]
    order = float(n_row * n_col * blocks[1] * blocks[2])
    extra = 6 if eta else 1
    any_space = pl.BlockSpec(memory_space=pl.ANY)
    vmem = pl.BlockSpec(memory_space=pltpu.VMEM)
    smem = pl.BlockSpec(memory_space=pltpu.SMEM)
    dma = pltpu.SemaphoreType.DMA
    width = max(n_row, n_col)
    return pl.pallas_call(
        functools.partial(kernel, eta, n_row, n_col, order),
        out_shape=(
            jax.ShapeDtypeStruct(density.shape, F32),
            jax.ShapeDtypeStruct(density.shape, F32),
            jax.ShapeDtypeStruct((2,), F32),
        ),
        in_specs=[smem, smem, any_space, any_space],
        out_specs=(vmem, vmem, smem),
        scratch_shapes=[
            pltpu.VMEM((7, 2, B, B), F32),
            pltpu.VMEM((7, 2, B, B), F32),
            pltpu.VMEM((8, 7, 2, B, B), F32),
            pltpu.VMEM((6, 6, 2, B, B), BF16),
            pltpu.VMEM((6, 6, 2, B, B), BF16),
            pltpu.VMEM((6, 6, 2, B, B), BF16),
            pltpu.VMEM((6, 6, 2, B, B), BF16),
            pltpu.VMEM((6, PACKED, B), F32),
            pltpu.VMEM((6, 4, PACKED, B), F32),
            pltpu.VMEM((2, 2, B, B), F32),
            pltpu.VMEM((7, 2, PACKED, B), F32),
            pltpu.VMEM((7, 2, PACKED, B), F32),
            pltpu.VMEM((7, 2, B, B), F32),
            pltpu.VMEM((extra, 3, 2, 2, B, B), F32),
            pltpu.VMEM((extra, 2, 2, B, B), F32),
            pltpu.VMEM((extra, 4, 2, B, B), F32),
            pltpu.VMEM((extra, 4, 2, B, B), F32),
            pltpu.VMEM((extra, 4, 2, B, B), BF16),
            pltpu.VMEM((extra, 4, 2, B, B), BF16),
            pltpu.VMEM((6, 2, B, B), F32),
            [pltpu.VMEM((2, 2, B, B), F32)] * extra,
            [pltpu.VMEM((2, 2, B, B), F32)] * extra,
            pltpu.VMEM((2, 2, 2, B), F32),
            pltpu.VMEM((2, 2, width, 2, B), F32),
            pltpu.SMEM((5, 8), I32),
            dma((2,)),
            dma((6, 4)),
            dma((6, 4)),
            dma((7, 2)),
            dma((7, 2)),
            dma((6, 8)),
            dma((6, 8)),
            dma((2, 2, width)),
            dma((2, 2, width)),
        ],
        compiler_params=pltpu.CompilerParams(
            collective_id=1 + eta, has_side_effects=True, vmem_limit_bytes=56 * 1024 * 1024
        ),
        name="sp2_" + ("mirrored", "open", "closed")[1 + eta],
    )(offsets.T, branch, density, hamiltonian)


def pattern_class(offsets):
    rows, cols, layers = offsets[:, 0], offsets[:, 1], offsets[:, 2] & 1
    kind = jnp.where(rows == 1, jnp.where(cols == 0, 1, jnp.where(cols == 1, 64, 512)), 8)
    leads = (rows == 1) | ((rows == 0) & (cols == 1))
    code = jnp.sum(jnp.where(leads, kind + (layers << 12), 0))
    seen, even = code & 4095, (code & 4096) == 0
    return jnp.where(even & (seen == 73), 1, jnp.where(even & (seen == 521), 2, 0)).astype(I32)


def solution(mesh):
    n_row, n_col = mesh.shape[ROW], mesh.shape[COL]

    def local(density, hamiltonian, offsets, branch):
        branches = [functools.partial(call, eta, n_row, n_col) for eta in (0, 1, -1)]
        return lax.switch(pattern_class(offsets), branches, density, hamiltonian, offsets, branch)

    spec = P(ROW, COL, None, None, None, None)
    return jax.shard_map(
        local, mesh=mesh, in_specs=(spec, spec, P(), P()), out_specs=(spec, spec, P()), check_vma=False
    )
```
